32 devices in a mesh: row: 4 (over z), col: 8 (over y, x, core).
Axes of the slice: x: 2, y: 2, z: 4, core: 2. Of those that a mesh axis runs over, the one named last changes fastest.
Arguments:
- velocity: bfloat16 [3, 4, 4128, 4096], P(None, None, 'row', 'col'), may hold values from -6 to 6
- rhs_prev: bfloat16 [3, 4, 4128, 4096], P(None, None, 'row', 'col'), may hold values from -12 to 12
- row_counts: int32 [4], replicated, may hold values from 1016 to 1032, as said below
- x_scale: float32 [4096], P('col'), may hold values from 0.5 to 2
- x_curv: float32 [4096], P('col'), may hold values from -3 to 3
- y_scale: float32 [4128], P('row'), may hold values from 0.5 to 12
- y_curv: float32 [4128], P('row'), may hold values from -3 to 3
- x_local: bfloat16 [516, 2, 512], replicated, may hold values from -0.25 to 0.25
- x_coupling: float32 [2, 16, 16], replicated, may hold values from -1.5 to 1.5
- x_basis: float32 [2, 2, 512], replicated, may hold values from -3 to 3
- y_local: bfloat16 [4144, 2, 1032], P('row'), may hold values from -0.1875 to 0.1875
- y_coupling: float32 [2, 8, 8], replicated, may hold values from -2 to 2
- y_basis: float32 [4, 2, 2, 1032], P('row'), may hold values from -3 to 3
Outputs:
- rhs: bfloat16 [3, 4, 4128, 4096], P(None, None, 'row', 'col')
- increment: bfloat16 [3, 4, 4128, 4096], P(None, None, 'row', 'col')
The draws below stay inside these ranges and needn't reach their ends.
Inputs may be any that keep to these rules, and one draw needn't show every extreme that they name: `row_counts`: the counts sum to 4097; each is at least 2, and the largest is exactly 1032.
All inputs are finite; a program needn't handle non-finite values.
Results may differ from the reference program's by a relative error of at most 0.0055.
Values may be sent and summed in bfloat16 or wider, within the bound.
A program may use at most 320 MiB of HBM per device.

```python
import math
import jax
import jax.numpy as jnp
from jax import lax

NX = 4096
NY = 4097
ZW = 4
XB = 512
SKEW = 8
YB = 1032
YP = 4128
N_ROW = 4
N_COL = 8


def draw_row_counts(key, part):
    base_rows = NY // N_ROW
    extra_rows = NY % N_ROW
    pick_key, roll_key = jax.random.split(jax.random.fold_in(key, 11))
    lift_ids = jax.random.randint(pick_key, (N_ROW,), 0, SKEW + 1)
    position = jnp.arange(N_ROW, dtype=jnp.int32)
    lift_ids = jnp.where(position == 0, SKEW, jnp.where(position == N_ROW - 1, 0, lift_ids))
    counts = base_rows + lift_ids - jnp.roll(lift_ids, 1) + jnp.where(position == 1, extra_rows, 0)
    roll_by = jax.random.randint(roll_key, (), 0, N_ROW)
    return jnp.roll(counts, roll_by).astype(jnp.int32)


def draw_y_scale(key, part):
    position = jnp.arange(YP, dtype=jnp.float32) / (YP - 1)
    jitter = jax.random.uniform(jax.random.fold_in(key, 5), (YP,), jnp.float32, 0.7, 1.3)
    return jnp.exp(jnp.log(4.0) * position) * jitter


def block_scale(rng, extent, pieces, smallest, high):
    loudness, own = 1.0, jax.random.fold_in(rng, 6)
    for dim, parts in pieces:
        heights = jnp.exp(jax.random.uniform(jax.random.fold_in(own, dim), (parts,), jnp.float32, smallest / len(pieces), high / len(pieces)))
        loudness = loudness * jnp.repeat(heights, extent[dim] // parts).reshape([-1 if axis == dim else 1 for axis in range(len(extent))])
    return loudness


def normal_values(rng, extent, width, limit, pieces=(), kind=jnp.bfloat16):
    factor_of = block_scale(rng, extent, pieces, -0.22, 0.18) if pieces else 1.0
    drawn = jax.random.normal(rng, extent, jnp.float32) * width * factor_of
    return jnp.minimum(jnp.maximum(drawn, -limit), limit).astype(kind)


def setup_inputs(seed: int = 0) -> dict:
    key_of = jax.random.split(jax.random.key(seed), 14)
    return {
        "velocity": normal_values(key_of[0], (3, ZW, YP, NX), 1.0, 6.0, ((2, 4), (3, 8))),
        "rhs_prev": normal_values(key_of[1], (3, ZW, YP, NX), 2.0, 12.0, ((2, 4), (3, 8))),
        "row_counts": draw_row_counts(jax.random.fold_in(key_of[13], 71), 0),
        "x_scale": jnp.clip(jnp.exp(math.log(2.0) - 1.3862944 * jax.random.uniform(key_of[3], (NX,), jnp.float32) ** block_scale(key_of[3], (NX,), ((0, 8),), -0.2, 0.2)), 0.5, 2.0),
        "x_curv": normal_values(key_of[4], (NX,), 0.5, 3.0, ((0, 8),), jnp.float32),
        "y_scale": draw_y_scale(jax.random.fold_in(key_of[13], 71), 0),
        "y_curv": normal_values(key_of[6], (YP,), 0.5, 3.0, ((0, 4),), jnp.float32),
        "x_local": normal_values(key_of[7], (XB + 4, 2, XB), (XB + 4) ** -0.5, 0.25),
        "x_coupling": normal_values(key_of[8], (2, 2 * N_COL, 2 * N_COL), (2 * N_COL) ** -0.5, 1.5, (), jnp.float32),
        "x_basis": normal_values(key_of[9], (2, 2, XB), 0.5, 3.0, (), jnp.float32),
        "y_local": normal_values(key_of[10], (N_ROW * (YB + 4), 2, YB), (YB + 4) ** -0.5, 0.1875, ((0, 4),)),
        "y_coupling": normal_values(key_of[11], (2, 2 * N_ROW, 2 * N_ROW), (2 * N_ROW) ** -0.5, 2.0, (), jnp.float32),
        "y_basis": normal_values(key_of[12], (N_ROW, 2, 2, YB), 0.5, 3.0, ((0, 4),), jnp.float32),
    }


viscosity = 0.1
cfl_target = 1.5
gamma_coef = 5.0 / 12.0
zeta_coef = -17.0 / 60.0


def x_derivs(fields_in, x_local, x_coupling, x_basis):
    x_width = NX // N_COL
    starts = jnp.arange(N_COL, dtype=jnp.int32) * x_width - 2
    gather_ids = (starts[:, None] + jnp.arange(x_width + 4, dtype=jnp.int32)[None, :]) % NX
    extended = fields_in[:, :, gather_ids]
    local_terms = jnp.dot(extended.reshape(-1, x_width + 4), x_local.reshape(x_width + 4, 2 * x_width), preferred_element_type=jnp.float32)
    local_terms = local_terms.reshape(3, YP, N_COL, 2, x_width)
    ends_x = jnp.stack([local_terms[..., 0], local_terms[..., x_width - 1]], axis=-1)
    ends_x = jnp.transpose(ends_x, (0, 1, 3, 2, 4)).reshape(3, YP, 2, 2 * N_COL)
    solved = jnp.einsum('kim,cykm->cyki', x_coupling, ends_x, precision=lax.Precision.HIGHEST)
    solved = jnp.transpose(solved.reshape(3, YP, 2, N_COL, 2), (0, 1, 3, 2, 4))
    result = local_terms + solved[..., 0:1] * x_basis[:, 0, :] + solved[..., 1:2] * x_basis[:, 1, :]
    first_x = result[:, :, :, 0, :].reshape(3, YP, NX)
    second_x = result[:, :, :, 1, :].reshape(3, YP, NX)
    return first_x, second_x


def y_derivs(masked, row_counts, y_local, y_coupling, y_basis):
    y_rows = YB
    blocks = jnp.arange(N_ROW, dtype=jnp.int32)
    below_counts = jnp.roll(row_counts, 1)
    offsets = jnp.arange(y_rows + 4, dtype=jnp.int32)
    low_ids = (blocks[:, None] - 1) * y_rows + below_counts[:, None] - 2 + offsets[None, :]
    mid_ids = blocks[:, None] * y_rows + offsets[None, :] - 2
    high_ids = (blocks[:, None] + 1) * y_rows + offsets[None, :] - y_rows - 2
    gather_ids = jnp.where(offsets[None, :] < 2, low_ids, jnp.where(offsets[None, :] < y_rows + 2, mid_ids, high_ids))
    keep_low = jnp.logical_or(offsets[None, :] >= 2, blocks[:, None] > 0)
    keep_high = jnp.logical_or(offsets[None, :] < y_rows + 2, blocks[:, None] < N_ROW - 1)
    keep_ids = jnp.logical_and(keep_low, keep_high)
    gather_ids = jnp.clip(gather_ids, 0, YP - 1).astype(jnp.int32)
    extended = jnp.where(keep_ids[None, :, :, None], masked[:, gather_ids, :], jnp.zeros((), masked.dtype))
    weights = y_local.reshape(N_ROW, y_rows + 4, 2 * y_rows).astype(jnp.float32)
    local_terms = jnp.einsum('qem,cqex->cqmx', weights, extended.astype(jnp.float32))
    local_terms = local_terms.reshape(3, N_ROW, 2, y_rows, NX)
    first_rows = local_terms[:, :, :, 0, :]
    last_rows = jnp.moveaxis(local_terms[:, blocks, :, row_counts - 1, :], 0, 1)
    ends_y = jnp.stack([first_rows, last_rows], axis=3)
    ends_y = jnp.transpose(ends_y, (0, 2, 1, 3, 4)).reshape(3, 2, 2 * N_ROW, NX)
    solved = jnp.einsum('kim,ckmx->ckix', y_coupling, ends_y, precision=lax.Precision.HIGHEST)
    solved = jnp.transpose(solved.reshape(3, 2, N_ROW, 2, NX), (0, 2, 1, 3, 4))
    result = local_terms + solved[:, :, :, 0, :][:, :, :, None, :] * y_basis[None, :, :, 0, :, None] + solved[:, :, :, 1, :][:, :, :, None, :] * y_basis[None, :, :, 1, :, None]
    first_y = result[:, :, 0].reshape(3, YP, NX)
    second_y = result[:, :, 1].reshape(3, YP, NX)
    return first_y, second_y


def reference(velocity, rhs_prev, row_counts, x_scale, x_curv, y_scale, y_curv, x_local, x_coupling, x_basis, y_local, y_coupling, y_basis):
    slot_ids = jnp.arange(YP, dtype=jnp.int32)
    valid_rows = (slot_ids % YB) < row_counts[slot_ids // YB]
    speeds = jnp.abs(velocity[0].astype(jnp.float32)) * x_scale + jnp.abs(velocity[1].astype(jnp.float32)) * y_scale[:, None]
    speed_top = jnp.max(jnp.where(valid_rows[:, None], speeds, jnp.float32(0.0)))
    time_step = cfl_target / (speed_top + 1e-6)
    scale_x = x_scale
    curve_x = x_curv
    scale_y = y_scale[:, None]
    curve_y = y_curv[:, None]

    def one_plane(plane_args):
        fields_in, previous = plane_args
        masked = jnp.where(valid_rows[None, :, None], fields_in, jnp.zeros((), fields_in.dtype))
        first_x, second_x = x_derivs(fields_in, x_local, x_coupling, x_basis)
        first_y, second_y = y_derivs(masked, row_counts, y_local, y_coupling, y_basis)
        velocity_f = fields_in.astype(jnp.float32)
        grad_x = scale_x * first_x
        grad_y = scale_y * first_y
        laplacian = scale_x * scale_x * second_x + curve_x * first_x + scale_y * scale_y * second_y + curve_y * first_y
        rhs_full = -(velocity_f[0:1] * grad_x + velocity_f[1:2] * grad_y) + viscosity * laplacian
        rhs_full = jnp.where(valid_rows[None, :, None], rhs_full, jnp.float32(0.0))
        change = time_step * (gamma_coef * rhs_full + zeta_coef * previous.astype(jnp.float32))
        change = jnp.where(valid_rows[None, :, None], change, jnp.float32(0.0))
        return rhs_full.astype(jnp.bfloat16), change.astype(jnp.bfloat16)

    fields = jnp.moveaxis(velocity, 1, 0)
    previous_rhs = jnp.moveaxis(rhs_prev, 1, 0)
    totals, changes = lax.map(one_plane, (fields, previous_rhs))
    return jnp.moveaxis(totals, 0, 1), jnp.moveaxis(changes, 0, 1)
```

```python
import functools
import jax
import jax.numpy as jnp
from jax import lax
from jax.experimental import pallas as pl
from jax.experimental.pallas import tpu as pltpu
from jax.sharding import PartitionSpec as P

viscosity = 0.1
cfl_target = 1.5
gamma_coef = 5.0 / 12.0
zeta_coef = -17.0 / 60.0
f32 = jnp.float32
bf16 = jnp.bfloat16


def dot(a, b, ca=1, cb=0):
    return lax.dot_general(a, b, (((ca,), (cb,)), ((), ())), preferred_element_type=f32)


def stats_kernel(vel, wx, wy, xs, ycol, xo, yo, top, xacc, yacc, peak):
    z = pl.program_id(0)
    speed = (
        jnp.abs(vel[0, 0].astype(f32)) * xs[...] + jnp.abs(vel[1, 0].astype(f32)) * ycol[:, 0:1]
    ) * ycol[:, 1:2]
    best = jnp.max(speed, axis=0, keepdims=True)
    for f in range(vel.shape[0]):
        block = vel[f, 0]
        px = dot(wx[0], block, 1, 1)
        py = dot(wy[0], block)

        @pl.when(z == 0)
        def _():
            xacc[f] = px
            yacc[f] = py

        @pl.when(z > 0)
        def _():
            xacc[f] = xacc[f] + px
            yacc[f] = yacc[f] + py

    @pl.when(z == 0)
    def _():
        peak[...] = best

    @pl.when(z > 0)
    def _():
        peak[...] = jnp.maximum(peak[...], best)

    @pl.when(z == pl.num_programs(0) - 1)
    def _():
        group = xo.shape[1] // vel.shape[0]
        for f in range(vel.shape[0]):
            for g in range(xo.shape[0]):
                xo[g, f * group : (f + 1) * group, :] = xacc[
                    f, g * group : (g + 1) * group, :
                ].astype(bf16)
            for g in range(yo.shape[0]):
                yo[g, f * group : (f + 1) * group, :] = yacc[
                    f, g * group : (g + 1) * group, :
                ].astype(bf16)
        top[...] = jnp.broadcast_to(jnp.max(peak[...], axis=1, keepdims=True), top.shape)


def exchange_kernel(n_row, n_col, xs, ys, top, xr, yr, tops, sx, rx, sy, ry, st, rt, su, ru, se, re, own):
    me_c = lax.axis_index("col")
    me_r = lax.axis_index("row")
    mesh_id = pl.DeviceIdType.MESH
    barrier = pltpu.get_barrier_semaphore()

    def at_col(d):
        return lax.rem(me_c + d, n_col)

    def at_row(d):
        return lax.rem(me_r + d, n_row)

    for d in range(1, n_col):
        pl.semaphore_signal(barrier, inc=1, device_id=(me_r, at_col(d)), device_id_type=mesh_id)
    for d in range(1, n_row):
        pl.semaphore_signal(barrier, inc=1, device_id=(at_row(d), me_c), device_id_type=mesh_id)
    pl.semaphore_wait(barrier, n_col + n_row - 2)

    def send(src, dst, ssem, rsem, device):
        copy = pltpu.make_async_remote_copy(
            src_ref=src, dst_ref=dst, send_sem=ssem, recv_sem=rsem, device_id=device, device_id_type=mesh_id
        )
        copy.start()
        return copy

    tcopies = [
        send(top, tops.at[me_r, me_c], st.at[d], rt.at[d], (me_r, at_col(d))) for d in range(1, n_col)
    ]
    own_t = pltpu.make_async_copy(top, tops.at[me_r, me_c], own.at[0])
    own_t.start()
    copies = []
    for d in range(1, n_col):
        peer = at_col(d)
        copies.append(send(xs.at[peer], xr.at[me_c], sx.at[d], rx.at[d], (me_r, peer)))
    copies.append(send(xs.at[n_col], xr.at[n_col], se.at[0], re.at[0], (me_r, at_col(1))))
    copies.append(
        send(xs.at[n_col + 1], xr.at[n_col + 1], se.at[1], re.at[1], (me_r, at_col(n_col - 1)))
    )
    for d in range(1, n_row):
        peer = at_row(d)
        copies.append(send(ys.at[peer], yr.at[me_r], sy.at[d], ry.at[d], (peer, me_c)))
    copies.append(send(ys.at[n_row], yr.at[n_row], se.at[2], re.at[2], (at_row(1), me_c)))
    copies.append(
        send(ys.at[n_row + 1], yr.at[n_row + 1], se.at[3], re.at[3], (at_row(n_row - 1), me_c))
    )
    own_x = pltpu.make_async_copy(xs.at[me_c], xr.at[me_c], own.at[1])
    own_y = pltpu.make_async_copy(ys.at[me_r], yr.at[me_r], own.at[2])
    own_x.start()
    own_y.start()
    own_t.wait()
    for copy in tcopies:
        copy.wait()
    ucopies = [
        send(tops.at[me_r], tops.at[me_r], su.at[d], ru.at[d], (at_row(d), me_c)) for d in range(1, n_row)
    ]
    own_x.wait()
    own_y.wait()
    for copy in copies + ucopies:
        copy.wait()


def main_kernel(main, tile, vel, prev, xr, yr, lx, bx, wy, wt, tops, ycol, rhs, inc, thin):
    f = pl.program_id(1)
    rows, width = prev.shape[2], prev.shape[3]
    top = jnp.max(tops[...], axis=(0, 1, 2))
    top = jnp.max(top.reshape(1, top.shape[0]), axis=1, keepdims=True)
    step = cfl_target / (top + 1e-06)
    thin_rows = yr.shape[0] * yr.shape[1]
    thin[0:thin_rows, :] = yr[...].reshape(thin_rows, width)
    if main < rows:
        thin[thin_rows : thin_rows + rows - main, :] = vel[f, 0, main:rows, :]
    lines = xr[...].reshape(xr.shape[0] * xr.shape[1], rows)
    starts = list(range(0, main, tile))
    for start in starts:
        stop = rows if start == starts[-1] else start + tile
        here = slice(start, stop)
        ax = dot(vel[f, 0, here, :], lx[...]) + dot(lines[:, here], bx[0], 0, 0)
        ay0 = dot(wy[0, here, :], vel[f, 0, 0:main, :]) + dot(wt[0, 0, here, :], thin[...])
        ay1 = dot(wy[1, here, :], vel[f, 0, 0:main, :]) + dot(wt[0, 1, here, :], thin[...])
        u = vel[0, 0, here, :].astype(f32)
        v = vel[1, 0, here, :].astype(f32)
        live = ycol[here, 1:2] > 0.0
        total = (ax[:, :width] + ay0) - (u * ax[:, width:] + v * ay1)
        total = jnp.where(live, total, 0.0)
        rhs[0, 0, here, :] = total.astype(bf16)
        change = step * (gamma_coef * total + zeta_coef * prev[0, 0, here, :].astype(f32))
        inc[0, 0, here, :] = jnp.where(live, change, 0.0).astype(bf16)


def per_plane(compact, planes):
    groups = compact.shape[0]
    eye = jnp.eye(planes, dtype=compact.dtype)
    eye = eye.reshape((planes, 1, planes, 1) + (1,) * (compact.ndim - 2))
    wide = compact[None, :, None] * eye
    return wide.reshape((planes, groups * planes * 4) + compact.shape[2:])


def source_weights(coupling, place, own_ends, next_ends, last_hot, prior_ends, first_hot):
    count = coupling.shape[1] // 2
    blocks = coupling.reshape(2, 2 * count, count, 2)

    def col(shift):
        at = lax.rem(place + shift + count, count)
        return lax.dynamic_index_in_dim(blocks, at, 2, keepdims=False)

    own, after, before = col(0), col(1), col(-1)
    total = jnp.zeros((), f32)
    for e in range(2):
        total = total + own[:, :, e, None] * own_ends[:, e, None, :]
        for h in range(2):
            total = total + after[:, :, e, None] * next_ends[h, :, e, None, None] * last_hot[h]
            total = total + before[:, :, e, None] * prior_ends[h, :, e, None, None] * first_hot[h]
    total = total.reshape(2, count, 2, total.shape[-1])
    return jnp.transpose(total, (1, 0, 2, 3)).reshape(count, 4, total.shape[-1])


def shards(
    velocity, rhs_prev, row_counts, x_scale, x_curv, y_scale, y_curv,
    x_local, x_coupling, x_basis, y_local, y_coupling, y_basis,
):
    n_comp, n_plane, rows, width = velocity.shape
    n_col, n_row = lax.axis_size("col"), lax.axis_size("row")
    col_pos, row_pos = lax.axis_index("col"), lax.axis_index("row")
    count = row_counts[row_pos]
    slots = jnp.arange(rows, dtype=jnp.int32)
    live = (slots < count).astype(f32)
    ycol = jnp.stack([y_scale, live], axis=1)

    at_ends = jnp.stack(
        [y_local[:, :, 0], lax.dynamic_index_in_dim(y_local, count - 1, 2, keepdims=False)], axis=2
    ).astype(f32)
    up = [(i, i + 1) for i in range(n_row - 1)]
    down = [(i + 1, i) for i in range(n_row - 1)]
    next_y = lax.ppermute(at_ends[0:2].astype(bf16), "row", down).astype(f32)
    prior_y = lax.ppermute(at_ends[rows + 2 : rows + 4].astype(bf16), "row", up).astype(f32)

    def hot(at, size):
        return (jnp.arange(size, dtype=jnp.int32) == at).astype(f32)

    def edge_groups(first, last):
        zero = jnp.zeros_like(first[0])
        return jnp.stack([jnp.stack(last + [zero, zero]), jnp.stack([zero, zero] + first)])

    first = [hot(h, width) for h in range(2)]
    last = [hot(width - 2 + h, width) for h in range(2)]
    xl = x_local.astype(f32)
    x_ends = jnp.stack([xl[:, :, 0], xl[:, :, width - 1]], axis=2)
    own_ends = jnp.transpose(x_ends[2 : width + 2], (1, 2, 0))
    wx = source_weights(x_coupling, col_pos, own_ends, x_ends[0:2], last, x_ends[width + 2 :], first)
    wx = per_plane(jnp.concatenate([wx, edge_groups(first, last)]), n_plane).astype(bf16)

    def fold_x(a):
        lap = viscosity * (x_scale * x_scale * a[..., 1, :] + x_curv * a[..., 0, :])
        return jnp.concatenate([lap, x_scale * a[..., 0, :]], axis=-1)

    lx_all = fold_x(xl)
    lx = lx_all[2 : width + 2].astype(bf16)
    by_k = jnp.eye(2, dtype=f32)[:, None, :, None]
    bx = fold_x((x_basis[:, :, None, :] * by_k).reshape(4, 2, width))
    zx = jnp.zeros((2, 2 * width), f32)
    bx = jnp.concatenate(
        [
            jnp.broadcast_to(bx, (n_col,) + bx.shape),
            jnp.stack([jnp.concatenate([lx_all[0:2], zx]), jnp.concatenate([zx, lx_all[width + 2 :]])]),
        ]
    )
    bx = per_plane(bx, n_plane).astype(bf16)

    first = [hot(h, rows) for h in range(2)]
    last = [hot(count - 2 + h, rows) for h in range(2)]
    own_ends = jnp.transpose(at_ends[2 : rows + 2], (1, 2, 0)) * live
    wyc = source_weights(y_coupling, row_pos, own_ends, next_y, last, prior_y, first)
    wyc = per_plane(jnp.concatenate([wyc, edge_groups(first, last)]), n_plane).astype(bf16)

    def fold_y(a):
        lap = viscosity * (y_scale * y_scale * a[..., 1, :] + y_curv * a[..., 0, :])
        return jnp.stack([lap, y_scale * a[..., 0, :]], axis=-2)

    yl = y_local.astype(f32)
    tail = rows % 128
    main = rows - tail
    ly = (fold_y(yl[2 : rows + 2]) * live[:, None, None]).astype(bf16)
    wy = jnp.transpose(ly[:main], (1, 2, 0))
    by = fold_y((y_basis[0][:, :, None, :] * by_k).reshape(4, 2, rows))
    zy = jnp.zeros((2, 2, rows), f32)
    low = fold_y(yl[0:2]) * (row_pos > 0).astype(f32)
    high = fold_y(yl[rows + 2 :]) * (row_pos < n_row - 1).astype(f32)
    by = jnp.concatenate(
        [
            jnp.broadcast_to(by, (n_row,) + by.shape),
            jnp.stack([jnp.concatenate([low, zy]), jnp.concatenate([zy, high])]),
        ]
    )
    by = per_plane(by, n_plane).astype(bf16)
    by = jnp.concatenate([by, jnp.broadcast_to(ly[main:], (n_plane,) + ly[main:].shape)], axis=1)
    wt = jnp.transpose(by, (0, 2, 3, 1))

    group = n_plane * 4
    gx, gy = n_col + 2, n_row + 2
    xs_row = x_scale.reshape(1, width)
    limit = 60 * 1024 * 1024
    whole = lambda shape: pl.BlockSpec(shape, lambda *i: (0,) * len(shape))
    by_plane = lambda shape: pl.BlockSpec((1,) + shape[1:], lambda z, *i: (z,) + (0,) * (len(shape) - 1))
    fields = pl.BlockSpec((n_comp, 1, rows, width), lambda z, *i: (0, z, 0, 0))
    xo, yo, top = pl.pallas_call(
        stats_kernel,
        name="stats",
        grid=(n_plane,),
        in_specs=[fields, by_plane(wx.shape), by_plane(wyc.shape), whole(xs_row.shape), whole(ycol.shape)],
        out_specs=[
            whole((gx, n_comp * group, rows)),
            whole((gy, n_comp * group, width)),
            whole((8, 128)),
        ],
        out_shape=[
            jax.ShapeDtypeStruct((gx, n_comp * group, rows), bf16),
            jax.ShapeDtypeStruct((gy, n_comp * group, width), bf16),
            jax.ShapeDtypeStruct((8, 128), f32),
        ],
        scratch_shapes=[
            pltpu.VMEM((n_comp, gx * group, rows), f32),
            pltpu.VMEM((n_comp, gy * group, width), f32),
            pltpu.VMEM((1, width), f32),
        ],
        compiler_params=pltpu.CompilerParams(vmem_limit_bytes=limit),
    )(velocity, wx, wyc, xs_row, ycol)

    dma = pltpu.SemaphoreType.DMA
    anywhere = pl.BlockSpec(memory_space=pl.ANY)
    xr, yr, tops = pl.pallas_call(
        functools.partial(exchange_kernel, n_row, n_col),
        name="exchange",
        in_specs=[anywhere] * 3,
        out_specs=[anywhere] * 3,
        out_shape=[
            jax.ShapeDtypeStruct(xo.shape, bf16),
            jax.ShapeDtypeStruct(yo.shape, bf16),
            jax.ShapeDtypeStruct((n_row, n_col, 8, 128), f32),
        ],
        scratch_shapes=[
            dma((n_col,)), dma((n_col,)), dma((n_row,)), dma((n_row,)), dma((n_col,)), dma((n_col,)),
            dma((n_row,)), dma((n_row,)), dma((4,)), dma((4,)), dma((3,)),
        ],
        compiler_params=pltpu.CompilerParams(collective_id=0, has_side_effects=True),
    )(xo, yo, top)

    one = pl.BlockSpec((1, 1, rows, width), lambda z, f: (f, z, 0, 0))
    tile = 256 if main >= 512 else main
    return pl.pallas_call(
        functools.partial(main_kernel, main, tile),
        name="sub_step",
        grid=(n_plane, n_comp),
        in_specs=[
            fields,
            one,
            pl.BlockSpec((gx, group, rows), lambda z, f: (0, f, 0)),
            pl.BlockSpec((gy, group, width), lambda z, f: (0, f, 0)),
            whole(lx.shape),
            by_plane(bx.shape),
            whole(wy.shape),
            by_plane(wt.shape),
            whole(tops.shape),
            whole(ycol.shape),
        ],
        out_specs=[one, one],
        out_shape=[jax.ShapeDtypeStruct(velocity.shape, bf16)] * 2,
        scratch_shapes=[pltpu.VMEM((gy * group + tail, width), bf16)],
        compiler_params=pltpu.CompilerParams(vmem_limit_bytes=limit),
    )(velocity, rhs_prev, xr, yr, lx, bx, wy, wt, tops, ycol)


def solution(mesh):
    placed = (
        P(None, None, "row", "col"),
        P(None, None, "row", "col"),
        P(),
        P("col"),
        P("col"),
        P("row"),
        P("row"),
        P(),
        P(),
        P(),
        P("row", None, None),
        P(),
        P("row", None, None, None),
    )
    return jax.shard_map(
        shards,
        mesh=mesh,
        in_specs=placed,
        out_specs=(P(None, None, "row", "col"), P(None, None, "row", "col")),
        check_vma=False,
    )
```

```python
import functools
import jax
import jax.numpy as jnp
import numpy as np
from jax import lax
from jax.experimental import pallas as pl
from jax.experimental.pallas import tpu as pltpu
from jax.sharding import PartitionSpec as P

viscosity = 0.1
cfl_target = 1.5
gamma_coef = 5.0 / 12.0
zeta_coef = -17.0 / 60.0
f32 = jnp.float32
bf16 = jnp.bfloat16


def dot(a, b, ca=1, cb=0):
    return lax.dot_general(a, b, (((ca,), (cb,)), ((), ())), preferred_element_type=f32)


def split(a):
    high = a.astype(bf16)
    return high, (a - high.astype(f32)).astype(bf16)


def combine(mix, parts):
    mh, ml = split(mix)
    ph, pw = split(parts)
    return dot(mh, ph) + dot(ml, ph) + dot(mh, pw)


def stats_kernel(vel, dx, dy, mx, my, xs, ycol, xo, yo, top, xg, yg, peak):
    z = pl.program_id(0)
    speed = (
        jnp.abs(vel[0, 0].astype(f32)) * xs[...] + jnp.abs(vel[1, 0].astype(f32)) * ycol[:, 0:1]
    ) * ycol[:, 1:2]
    best = jnp.max(speed, axis=0, keepdims=True)
    for f in range(vel.shape[0]):
        block = vel[f, 0]
        xg[f, z] = dot(dx[...], block, 1, 1)
        yg[f, z] = dot(dy[...], block)

    @pl.when(z == 0)
    def _():
        peak[...] = best

    @pl.when(z > 0)
    def _():
        peak[...] = jnp.maximum(peak[...], best)

    @pl.when(z == pl.num_programs(0) - 1)
    def _():
        group = xo.shape[1] // vel.shape[0]
        for f in range(vel.shape[0]):
            for out, mix, parts in ((xo, mx, xg), (yo, my, yg)):
                flat = parts[f].reshape(parts.shape[1] * 8, parts.shape[3])
                total = combine(mix[...], flat).astype(bf16)
                out[:, f * group : (f + 1) * group, :] = total.reshape(
                    out.shape[0], group, out.shape[2]
                )
        top[...] = jnp.broadcast_to(jnp.max(peak[...], axis=1, keepdims=True), top.shape)


def prepare(xt, yt, xrow, ycol, livek, bx8, by8, sx, s1, s2, s3, lx, bx, wy, wt):
    width = xt.shape[2]
    rows, main = wy.shape[1], wy.shape[2]
    planes, thin = wt.shape[0], wt.shape[3]
    a0 = xt[0].astype(f32)
    a1 = xt[1].astype(f32)
    xs, xc = xrow[0:1, :], xrow[1:2, :]
    lx[:, :width] = (viscosity * (xs * xs * a1 + xc * a0))[2 : width + 2].astype(bf16)
    lx[:, width:] = (xs * a0)[2 : width + 2].astype(bf16)
    bx[...] = dot(sx[...], bx8[...].astype(bf16)).astype(bf16).reshape(bx.shape)
    starts = list(range(0, main, 128))
    for start in starts:
        stop = rows if start == starts[-1] else start + 128
        here = slice(start, stop)
        b0 = yt[0, here, :].astype(f32) * livek[...]
        b1 = yt[1, here, :].astype(f32) * livek[...]
        ys, yc = ycol[here, 0:1], ycol[here, 2:3]
        for q, fold in enumerate((viscosity * (ys * ys * b1 + yc * b0), ys * b0)):
            wy[q, here, :] = fold[:, 2 : main + 2].astype(bf16)
            small = fold.astype(bf16)
            wide = (
                dot(by8[q, :, here].astype(bf16), s1[...], 0, 0)
                + dot(small[:, 0:128], s2[...])
                + dot(small[:, main:], s3[...])
            ).astype(bf16)
            for z in range(planes):
                wt[z, q, here, :] = wide[:, z * thin : (z + 1) * thin]


def exchange_kernel(n_row, n_col, *refs):
    xs, ys, top = refs[:3]
    sources = refs[3:14]
    xr, yr, tops = refs[14:17]
    weights = refs[17:21]
    sx, rx, sy, ry, st, rt, su, ru, se, re, own = refs[21:]
    me_c = lax.axis_index("col")
    me_r = lax.axis_index("row")
    mesh_id = pl.DeviceIdType.MESH
    barrier = pltpu.get_barrier_semaphore()

    def at_col(d):
        return lax.rem(me_c + d, n_col)

    def at_row(d):
        return lax.rem(me_r + d, n_row)

    for d in range(1, n_col):
        pl.semaphore_signal(barrier, inc=1, device_id=(me_r, at_col(d)), device_id_type=mesh_id)
    for d in range(1, n_row):
        pl.semaphore_signal(barrier, inc=1, device_id=(at_row(d), me_c), device_id_type=mesh_id)
    pl.semaphore_wait(barrier, n_col + n_row - 2)

    def send(src, dst, ssem, rsem, device):
        copy = pltpu.make_async_remote_copy(
            src_ref=src, dst_ref=dst, send_sem=ssem, recv_sem=rsem, device_id=device, device_id_type=mesh_id
        )
        copy.start()
        return copy

    tcopies = [
        send(top, tops.at[me_r, me_c], st.at[d], rt.at[d], (me_r, at_col(d))) for d in range(1, n_col)
    ]
    own_t = pltpu.make_async_copy(top, tops.at[me_r, me_c], own.at[0])
    own_t.start()
    copies = []
    for d in range(1, n_col):
        peer = at_col(d)
        copies.append(send(xs.at[peer], xr.at[me_c], sx.at[d], rx.at[d], (me_r, peer)))
    copies.append(send(xs.at[n_col], xr.at[n_col], se.at[0], re.at[0], (me_r, at_col(1))))
    copies.append(
        send(xs.at[n_col + 1], xr.at[n_col + 1], se.at[1], re.at[1], (me_r, at_col(n_col - 1)))
    )
    for d in range(1, n_row):
        peer = at_row(d)
        copies.append(send(ys.at[peer], yr.at[me_r], sy.at[d], ry.at[d], (peer, me_c)))
    copies.append(send(ys.at[n_row], yr.at[n_row], se.at[2], re.at[2], (at_row(1), me_c)))
    copies.append(
        send(ys.at[n_row + 1], yr.at[n_row + 1], se.at[3], re.at[3], (at_row(n_row - 1), me_c))
    )
    own_x = pltpu.make_async_copy(xs.at[me_c], xr.at[me_c], own.at[1])
    own_y = pltpu.make_async_copy(ys.at[me_r], yr.at[me_r], own.at[2])
    own_x.start()
    own_y.start()
    own_t.wait()
    for copy in tcopies:
        copy.wait()
    ucopies = [
        send(tops.at[me_r], tops.at[me_r], su.at[d], ru.at[d], (at_row(d), me_c)) for d in range(1, n_row)
    ]
    prepare(*sources, *weights)
    own_x.wait()
    own_y.wait()
    for copy in copies + ucopies:
        copy.wait()


def main_kernel(main, tile, vel, prev, xr, yr, lx, bx, wy, wt, tops, ycol, rhs, inc, thin):
    f = pl.program_id(1)
    rows, width = prev.shape[2], prev.shape[3]
    top = jnp.max(tops[...], axis=(0, 1, 2))
    top = jnp.max(top.reshape(1, top.shape[0]), axis=1, keepdims=True)
    step = cfl_target / (top + 1e-06)
    thin_rows = yr.shape[0] * yr.shape[1]
    thin[0:thin_rows, :] = yr[...].reshape(thin_rows, width)
    if main < rows:
        thin[thin_rows : thin_rows + rows - main, :] = vel[f, 0, main:rows, :]
    filled = thin_rows + rows - main
    if filled < thin.shape[0]:
        thin[filled:, :] = jnp.zeros((thin.shape[0] - filled, width), bf16)
    lines = xr[...].reshape(xr.shape[0] * xr.shape[1], rows)
    starts = list(range(0, main, tile))
    for start in starts:
        stop = rows if start == starts[-1] else start + tile
        here = slice(start, stop)
        ax = dot(vel[f, 0, here, :], lx[...]) + dot(lines[:, here], bx[0], 0, 0)
        ay0 = dot(wy[0, here, :], vel[f, 0, 0:main, :]) + dot(wt[0, 0, here, :], thin[...])
        ay1 = dot(wy[1, here, :], vel[f, 0, 0:main, :]) + dot(wt[0, 1, here, :], thin[...])
        u = vel[0, 0, here, :].astype(f32)
        v = vel[1, 0, here, :].astype(f32)
        live = ycol[here, 1:2] > 0.0
        total = (ax[:, :width] + ay0) - (u * ax[:, width:] + v * ay1)
        total = jnp.where(live, total, 0.0)
        rhs[0, 0, here, :] = total.astype(bf16)
        change = step * (gamma_coef * total + zeta_coef * prev[0, 0, here, :].astype(f32))
        inc[0, 0, here, :] = jnp.where(live, change, 0.0).astype(bf16)


def source_mix(coupling, place, next_ends, prior_ends, planes):
    count = coupling.shape[1] // 2
    blocks = coupling.reshape(2, 2 * count, count, 2)

    def col(shift):
        at = lax.rem(place + shift + count, count)
        return lax.dynamic_index_in_dim(blocks, at, 2, keepdims=False)

    own = col(0)[:, :, None, :] * jnp.eye(2, dtype=f32)[:, None, :, None]
    own = own.reshape(2, 2 * count, 4)
    first = jnp.sum(col(-1)[:, :, None, :] * jnp.transpose(prior_ends, (1, 0, 2))[:, None], axis=3)
    last = jnp.sum(col(1)[:, :, None, :] * jnp.transpose(next_ends, (1, 0, 2))[:, None], axis=3)
    mix = jnp.concatenate([own, first, last], axis=2).reshape(2, count, 2, 8)
    mix = jnp.transpose(mix, (1, 0, 2, 3)).reshape(count, 4, 8)
    edges = np.zeros((2, 4, 8), np.float32)
    edges[0, 0, 6] = edges[0, 1, 7] = edges[1, 2, 4] = edges[1, 3, 5] = 1.0
    mix = jnp.concatenate([mix, edges])
    wide = mix[:, None, :, None, :] * np.eye(planes, dtype=np.float32)[None, :, None, :, None]
    return wide.reshape((count + 2) * planes * 4, planes * 8)


def shards(
    velocity, rhs_prev, row_counts, x_scale, x_curv, y_scale, y_curv,
    x_local, x_coupling, x_basis, y_local, y_coupling, y_basis,
):
    n_comp, n_plane, rows, width = velocity.shape
    n_col, n_row = lax.axis_size("col"), lax.axis_size("row")
    col_pos, row_pos = lax.axis_index("col"), lax.axis_index("row")
    group = n_plane * 4
    gx, gy = n_col + 2, n_row + 2
    tail = rows % 128
    main = rows - tail
    count = row_counts[row_pos]
    slots = jnp.arange(rows, dtype=jnp.int32)
    live = (slots < count).astype(f32)
    ycol = jnp.stack([y_scale, live, y_curv], axis=1)
    yt = jnp.transpose(y_local, (1, 2, 0))
    xt = jnp.transpose(x_local, (1, 0, 2))

    y_ends = jnp.stack(
        [yt[:, 0, :], lax.dynamic_index_in_dim(yt, count - 1, 1, keepdims=False)], axis=1
    )
    up = [(i, i + 1) for i in range(n_row - 1)]
    down = [(i + 1, i) for i in range(n_row - 1)]
    next_y = lax.ppermute(y_ends[:, :, 0:2], "row", down).astype(f32)
    prior_y = lax.ppermute(y_ends[:, :, rows + 2 :], "row", up).astype(f32)
    x_ends = jnp.stack([x_local[:, :, 0], x_local[:, :, width - 1]], axis=2)
    x_ends_f = x_ends.astype(f32)

    def hot(at, size):
        return (jnp.arange(size, dtype=jnp.int32) == at).astype(bf16)

    dx = jnp.concatenate(
        [
            jnp.transpose(x_ends[2 : width + 2], (1, 2, 0)).reshape(4, width),
            jnp.stack([hot(0, width), hot(1, width), hot(width - 2, width), hot(width - 1, width)]),
        ]
    )
    dy = jnp.concatenate(
        [
            (y_ends[:, :, 2 : rows + 2] * live.astype(bf16)).reshape(4, rows),
            jnp.stack([hot(0, rows), hot(1, rows), hot(count - 2, rows), hot(count - 1, rows)]),
        ]
    )
    mx = source_mix(x_coupling, col_pos, x_ends_f[0:2], x_ends_f[width + 2 :], n_plane)
    my = source_mix(
        y_coupling, row_pos, jnp.transpose(next_y, (2, 0, 1)), jnp.transpose(prior_y, (2, 0, 1)), n_plane
    )

    def fold_x(a0, a1):
        lap = viscosity * (x_scale * x_scale * a1 + x_curv * a0)
        return jnp.concatenate([lap, x_scale * a0], axis=-1)

    def fold_y(a0, a1):
        return jnp.stack([viscosity * (y_scale * y_scale * a1 + y_curv * a0), y_scale * a0])

    def by_k(basis):
        zero = jnp.zeros_like(basis[0])
        return jnp.concatenate([basis[0], zero]), jnp.concatenate([zero, basis[1]])

    edge = jnp.concatenate([xt[:, 0:2], xt[:, width + 2 :]], axis=1).astype(f32)
    x0, x1 = by_k(x_basis)
    bx8 = fold_x(jnp.concatenate([x0, edge[0]]), jnp.concatenate([x1, edge[1]]))
    y0, y1 = by_k(y_basis[0])
    by8 = jnp.pad(fold_y(y0, y1), ((0, 0), (0, 4), (0, 0)))
    place = jnp.arange(rows + 4, dtype=jnp.int32) - 2
    livek = jnp.logical_and(place < count, jnp.logical_or(place >= 0, row_pos > 0))
    livek = jnp.logical_or(livek, jnp.logical_and(place >= rows, row_pos < n_row - 1))
    livek = livek.astype(f32)[None, :]
    xrow = jnp.stack([x_scale, x_curv])

    thin = -(-(gy * group + tail) // 128) * 128
    sx = np.zeros((n_plane, gx, n_plane, 4, 8), np.float32)
    s1 = np.zeros((8, n_plane, thin), np.float32)
    s2 = np.zeros((128, n_plane, thin), np.float32)
    s3 = np.zeros((tail + 4, n_plane, thin), np.float32)
    for z in range(n_plane):
        for c in range(4):
            sx[z, :n_col, z, c, c] = 1.0
            s1[c, z, np.arange(n_row) * group + z * 4 + c] = 1.0
        for h in range(2):
            sx[z, n_col, z, h, 4 + h] = 1.0
            sx[z, n_col + 1, z, 2 + h, 6 + h] = 1.0
            s2[h, z, n_row * group + z * 4 + h] = 1.0
            s3[tail + 2 + h, z, (n_row + 1) * group + z * 4 + 2 + h] = 1.0
        for t in range(tail):
            s3[2 + t, z, gy * group + t] = 1.0
    sx = jnp.asarray(sx.reshape(-1, 8), bf16)
    s1, s2, s3 = (jnp.asarray(s.reshape(s.shape[0], -1), bf16) for s in (s1, s2, s3))

    xs_row = x_scale.reshape(1, width)
    limit = 60 * 1024 * 1024
    whole = lambda shape: pl.BlockSpec(shape, lambda *i: (0,) * len(shape))
    by_plane = lambda shape: pl.BlockSpec((1,) + shape[1:], lambda z, *i: (z,) + (0,) * (len(shape) - 1))
    fields = pl.BlockSpec((n_comp, 1, rows, width), lambda z, *i: (0, z, 0, 0))
    xo, yo, top = pl.pallas_call(
        stats_kernel,
        name="stats",
        grid=(n_plane,),
        in_specs=[fields] + [whole(a.shape) for a in (dx, dy, mx, my, xs_row, ycol)],
        out_specs=[
            whole((gx, n_comp * group, rows)),
            whole((gy, n_comp * group, width)),
            whole((8, 128)),
        ],
        out_shape=[
            jax.ShapeDtypeStruct((gx, n_comp * group, rows), bf16),
            jax.ShapeDtypeStruct((gy, n_comp * group, width), bf16),
            jax.ShapeDtypeStruct((8, 128), f32),
        ],
        scratch_shapes=[
            pltpu.VMEM((n_comp, n_plane, 8, rows), f32),
            pltpu.VMEM((n_comp, n_plane, 8, width), f32),
            pltpu.VMEM((1, width), f32),
        ],
        compiler_params=pltpu.CompilerParams(vmem_limit_bytes=limit),
    )(velocity, dx, dy, mx, my, xs_row, ycol)

    dma = pltpu.SemaphoreType.DMA
    anywhere = pl.BlockSpec(memory_space=pl.ANY)
    in_vmem = pl.BlockSpec(memory_space=pltpu.VMEM)
    sources = (xt, yt, xrow, ycol, livek, bx8, by8, sx, s1, s2, s3)
    xr, yr, tops, lx, bx, wy, wt = pl.pallas_call(
        functools.partial(exchange_kernel, n_row, n_col),
        name="exchange",
        in_specs=[anywhere] * 3 + [in_vmem] * len(sources),
        out_specs=[anywhere] * 3 + [in_vmem] * 4,
        out_shape=[
            jax.ShapeDtypeStruct(xo.shape, bf16),
            jax.ShapeDtypeStruct(yo.shape, bf16),
            jax.ShapeDtypeStruct((n_row, n_col, 8, 128), f32),
            jax.ShapeDtypeStruct((width, 2 * width), bf16),
            jax.ShapeDtypeStruct((n_plane, gx * group, 2 * width), bf16),
            jax.ShapeDtypeStruct((2, rows, main), bf16),
            jax.ShapeDtypeStruct((n_plane, 2, rows, thin), bf16),
        ],
        scratch_shapes=[
            dma((n_col,)), dma((n_col,)), dma((n_row,)), dma((n_row,)), dma((n_col,)), dma((n_col,)),
            dma((n_row,)), dma((n_row,)), dma((4,)), dma((4,)), dma((3,)),
        ],
        compiler_params=pltpu.CompilerParams(
            collective_id=0, has_side_effects=True, vmem_limit_bytes=limit
        ),
    )(xo, yo, top, *sources)

    one = pl.BlockSpec((1, 1, rows, width), lambda z, f: (f, z, 0, 0))
    tile = 256 if main >= 512 else main
    return pl.pallas_call(
        functools.partial(main_kernel, main, tile),
        name="sub_step",
        grid=(n_plane, n_comp),
        in_specs=[
            fields,
            one,
            pl.BlockSpec((gx, group, rows), lambda z, f: (0, f, 0)),
            pl.BlockSpec((gy, group, width), lambda z, f: (0, f, 0)),
            whole(lx.shape),
            by_plane(bx.shape),
            whole(wy.shape),
            by_plane(wt.shape),
            whole(tops.shape),
            whole(ycol.shape),
        ],
        out_specs=[one, one],
        out_shape=[jax.ShapeDtypeStruct(velocity.shape, bf16)] * 2,
        scratch_shapes=[pltpu.VMEM((thin, width), bf16)],
        compiler_params=pltpu.CompilerParams(vmem_limit_bytes=limit),
    )(velocity, rhs_prev, xr, yr, lx, bx, wy, wt, tops, ycol)


def solution(mesh):
    placed = (
        P(None, None, "row", "col"),
        P(None, None, "row", "col"),
        P(),
        P("col"),
        P("col"),
        P("row"),
        P("row"),
        P(),
        P(),
        P(),
        P("row", None, None),
        P(),
        P("row", None, None, None),
    )
    return jax.shard_map(
        shards,
        mesh=mesh,
        in_specs=placed,
        out_specs=(P(None, None, "row", "col"), P(None, None, "row", "col")),
        check_vma=False,
    )
```

```python
import functools
import jax
import jax.numpy as jnp
import numpy as np
from jax import lax
from jax.experimental import pallas as pl
from jax.experimental.pallas import tpu as pltpu
from jax.sharding import PartitionSpec as P

viscosity = 0.1
cfl_target = 1.5
gamma_coef = 5.0 / 12.0
zeta_coef = -17.0 / 60.0
f32 = jnp.float32
bf16 = jnp.bfloat16


def dot(a, b, ca=1, cb=0):
    return lax.dot_general(a, b, (((ca,), (cb,)), ((), ())), preferred_element_type=f32)


def split(a):
    high = a.astype(bf16)
    return high, (a - high.astype(f32)).astype(bf16)


def combine(mix, parts):
    mh, ml = split(mix)
    ph, pw = split(parts)
    return dot(mh, ph) + dot(ml, ph) + dot(mh, pw)


def stats_kernel(vel, dx, dy, mx, my, xs, ycol, xo, yo, top, xg, yg, peak):
    z = pl.program_id(0)
    speed = (
        jnp.abs(vel[0, 0].astype(f32)) * xs[...] + jnp.abs(vel[1, 0].astype(f32)) * ycol[:, 0:1]
    ) * ycol[:, 1:2]
    best = jnp.max(speed, axis=0, keepdims=True)
    for f in range(vel.shape[0]):
        block = vel[f, 0]
        xg[f, z] = dot(dx[...], block, 1, 1)
        yg[f, z] = dot(dy[...], block)

    @pl.when(z == 0)
    def _():
        peak[...] = best

    @pl.when(z > 0)
    def _():
        peak[...] = jnp.maximum(peak[...], best)

    @pl.when(z == pl.num_programs(0) - 1)
    def _():
        group = xo.shape[1] // vel.shape[0]
        for f in range(vel.shape[0]):
            for out, mix, parts in ((xo, mx, xg), (yo, my, yg)):
                flat = parts[f].reshape(parts.shape[1] * 8, parts.shape[3])
                total = combine(mix[...], flat).astype(bf16)
                out[:, f * group : (f + 1) * group, :] = total.reshape(
                    out.shape[0], group, out.shape[2]
                )
        top[...] = jnp.broadcast_to(jnp.max(peak[...], axis=1, keepdims=True), top.shape)


def prepare(xt, yt, xrow, ycol, livek, bx8, by8, sx, s1, s2, s3, lx, bx, wy, wt):
    width = xt.shape[2]
    rows, main = wy.shape[1], wy.shape[2]
    planes, thin = wt.shape[0], wt.shape[3]
    a0 = xt[0].astype(f32)
    a1 = xt[1].astype(f32)
    xs, xc = xrow[0:1, :], xrow[1:2, :]
    lx[:, :width] = (viscosity * (xs * xs * a1 + xc * a0))[2 : width + 2].astype(bf16)
    lx[:, width:] = (xs * a0)[2 : width + 2].astype(bf16)
    bx[...] = dot(sx[...], bx8[...].astype(bf16)).astype(bf16).reshape(bx.shape)
    starts = list(range(0, main, 128))
    for start in starts:
        stop = rows if start == starts[-1] else start + 128
        here = slice(start, stop)
        b0 = yt[0, here, :].astype(f32) * livek[...]
        b1 = yt[1, here, :].astype(f32) * livek[...]
        ys, yc = ycol[here, 0:1], ycol[here, 2:3]
        for q, fold in enumerate((viscosity * (ys * ys * b1 + yc * b0), ys * b0)):
            wy[q, here, :] = fold[:, 2 : main + 2].astype(bf16)
            small = fold.astype(bf16)
            wide = (
                dot(by8[q, :, here].astype(bf16), s1[...], 0, 0)
                + dot(small[:, 0:128], s2[...])
                + dot(small[:, main:], s3[...])
            ).astype(bf16)
            for z in range(planes):
                wt[z, q, here, :] = wide[:, z * thin : (z + 1) * thin]


def exchange_kernel(n_row, n_col, *refs):
    xs, ys, top = refs[:3]
    sources = refs[3:14]
    xr, yr, tops = refs[14:17]
    weights = refs[17:21]
    sx, rx, sy, ry, st, rt, su, ru, se, re, own = refs[21:]
    me_c = lax.axis_index("col")
    me_r = lax.axis_index("row")
    mesh_id = pl.DeviceIdType.MESH
    barrier = pltpu.get_barrier_semaphore()

    def at_col(d):
        return lax.rem(me_c + d, n_col)

    def at_row(d):
        return lax.rem(me_r + d, n_row)

    for d in range(1, n_col):
        pl.semaphore_signal(barrier, inc=1, device_id=(me_r, at_col(d)), device_id_type=mesh_id)
    for d in range(1, n_row):
        pl.semaphore_signal(barrier, inc=1, device_id=(at_row(d), me_c), device_id_type=mesh_id)
    pl.semaphore_wait(barrier, n_col + n_row - 2)

    def send(src, dst, ssem, rsem, device):
        copy = pltpu.make_async_remote_copy(
            src_ref=src, dst_ref=dst, send_sem=ssem, recv_sem=rsem, device_id=device, device_id_type=mesh_id
        )
        copy.start()
        return copy

    tcopies = [
        send(top, tops.at[me_r, me_c], st.at[d], rt.at[d], (me_r, at_col(d))) for d in range(1, n_col)
    ]
    own_t = pltpu.make_async_copy(top, tops.at[me_r, me_c], own.at[0])
    own_t.start()
    copies = []
    for d in range(1, n_col):
        peer = at_col(d)
        copies.append(send(xs.at[peer], xr.at[me_c], sx.at[d], rx.at[d], (me_r, peer)))
    copies.append(send(xs.at[n_col], xr.at[n_col], se.at[0], re.at[0], (me_r, at_col(1))))
    copies.append(
        send(xs.at[n_col + 1], xr.at[n_col + 1], se.at[1], re.at[1], (me_r, at_col(n_col - 1)))
    )
    for d in range(1, n_row):
        peer = at_row(d)
        copies.append(send(ys.at[peer], yr.at[me_r], sy.at[d], ry.at[d], (peer, me_c)))
    copies.append(send(ys.at[n_row], yr.at[n_row], se.at[2], re.at[2], (at_row(1), me_c)))
    copies.append(
        send(ys.at[n_row + 1], yr.at[n_row + 1], se.at[3], re.at[3], (at_row(n_row - 1), me_c))
    )
    own_x = pltpu.make_async_copy(xs.at[me_c], xr.at[me_c], own.at[1])
    own_y = pltpu.make_async_copy(ys.at[me_r], yr.at[me_r], own.at[2])
    own_x.start()
    own_y.start()
    own_t.wait()
    for copy in tcopies:
        copy.wait()
    ucopies = [
        send(tops.at[me_r], tops.at[me_r], su.at[d], ru.at[d], (at_row(d), me_c)) for d in range(1, n_row)
    ]
    prepare(*sources, *weights)
    own_x.wait()
    own_y.wait()
    for copy in copies + ucopies:
        copy.wait()


def main_kernel(main, tile, vel, prev, xr, yr, lx, bx, wy, wt, tops, ycol, rhs, inc, thin):
    f = pl.program_id(1)
    rows, width = prev.shape[2], prev.shape[3]
    top = jnp.max(tops[...], axis=(0, 1, 2))
    top = jnp.max(top.reshape(1, top.shape[0]), axis=1, keepdims=True)
    step = cfl_target / (top + 1e-06)
    thin_rows = yr.shape[0] * yr.shape[1]
    thin[0:thin_rows, :] = yr[...].reshape(thin_rows, width)
    if main < rows:
        thin[thin_rows : thin_rows + rows - main, :] = vel[f, 0, main:rows, :]
    filled = thin_rows + rows - main
    if filled < thin.shape[0]:
        thin[filled:, :] = jnp.zeros((thin.shape[0] - filled, width), bf16)
    lines = xr[...].reshape(xr.shape[0] * xr.shape[1], rows)
    across = jnp.concatenate([lx[...], bx[0]], axis=0)
    along = jnp.concatenate([vel[f, 0, 0:main, :], thin[...]], axis=0)
    starts = list(range(0, main, tile))
    for start in starts:
        stop = rows if start == starts[-1] else start + tile
        here = slice(start, stop)
        points = jnp.concatenate([vel[f, 0, here, :], lines[:, here].T], axis=1)
        ax = dot(points, across)
        ay0 = dot(jnp.concatenate([wy[0, here, :], wt[0, 0, here, :]], axis=1), along)
        ay1 = dot(jnp.concatenate([wy[1, here, :], wt[0, 1, here, :]], axis=1), along)
        u = vel[0, 0, here, :].astype(f32)
        v = vel[1, 0, here, :].astype(f32)
        live = ycol[here, 1:2] > 0.0
        total = (ax[:, :width] + ay0) - (u * ax[:, width:] + v * ay1)
        total = jnp.where(live, total, 0.0)
        rhs[0, 0, here, :] = total.astype(bf16)
        change = step * (gamma_coef * total + zeta_coef * prev[0, 0, here, :].astype(f32))
        inc[0, 0, here, :] = jnp.where(live, change, 0.0).astype(bf16)


def source_mix(coupling, place, next_ends, prior_ends, planes):
    count = coupling.shape[1] // 2
    blocks = coupling.reshape(2, 2 * count, count, 2)

    def col(shift):
        at = lax.rem(place + shift + count, count)
        return lax.dynamic_index_in_dim(blocks, at, 2, keepdims=False)

    own = col(0)[:, :, None, :] * jnp.eye(2, dtype=f32)[:, None, :, None]
    own = own.reshape(2, 2 * count, 4)
    first = jnp.sum(col(-1)[:, :, None, :] * jnp.transpose(prior_ends, (1, 0, 2))[:, None], axis=3)
    last = jnp.sum(col(1)[:, :, None, :] * jnp.transpose(next_ends, (1, 0, 2))[:, None], axis=3)
    mix = jnp.concatenate([own, first, last], axis=2).reshape(2, count, 2, 8)
    mix = jnp.transpose(mix, (1, 0, 2, 3)).reshape(count, 4, 8)
    edges = np.zeros((2, 4, 8), np.float32)
    edges[0, 0, 6] = edges[0, 1, 7] = edges[1, 2, 4] = edges[1, 3, 5] = 1.0
    mix = jnp.concatenate([mix, edges])
    wide = mix[:, None, :, None, :] * np.eye(planes, dtype=np.float32)[None, :, None, :, None]
    return wide.reshape((count + 2) * planes * 4, planes * 8)


def shards(
    velocity, rhs_prev, row_counts, x_scale, x_curv, y_scale, y_curv,
    x_local, x_coupling, x_basis, y_local, y_coupling, y_basis,
):
    n_comp, n_plane, rows, width = velocity.shape
    n_col, n_row = lax.axis_size("col"), lax.axis_size("row")
    col_pos, row_pos = lax.axis_index("col"), lax.axis_index("row")
    group = n_plane * 4
    gx, gy = n_col + 2, n_row + 2
    tail = rows % 128
    main = rows - tail
    count = row_counts[row_pos]
    slots = jnp.arange(rows, dtype=jnp.int32)
    live = (slots < count).astype(f32)
    ycol = jnp.stack([y_scale, live, y_curv], axis=1)
    yt = jnp.transpose(y_local, (1, 2, 0))
    xt = jnp.transpose(x_local, (1, 0, 2))

    y_ends = jnp.stack(
        [yt[:, 0, :], lax.dynamic_index_in_dim(yt, count - 1, 1, keepdims=False)], axis=1
    )
    up = [(i, i + 1) for i in range(n_row - 1)]
    down = [(i + 1, i) for i in range(n_row - 1)]
    next_y = lax.ppermute(y_ends[:, :, 0:2], "row", down).astype(f32)
    prior_y = lax.ppermute(y_ends[:, :, rows + 2 :], "row", up).astype(f32)
    x_ends = jnp.stack([x_local[:, :, 0], x_local[:, :, width - 1]], axis=2)
    x_ends_f = x_ends.astype(f32)

    def hot(at, size):
        return (jnp.arange(size, dtype=jnp.int32) == at).astype(bf16)

    dx = jnp.concatenate(
        [
            jnp.transpose(x_ends[2 : width + 2], (1, 2, 0)).reshape(4, width),
            jnp.stack([hot(0, width), hot(1, width), hot(width - 2, width), hot(width - 1, width)]),
        ]
    )
    dy = jnp.concatenate(
        [
            (y_ends[:, :, 2 : rows + 2] * live.astype(bf16)).reshape(4, rows),
            jnp.stack([hot(0, rows), hot(1, rows), hot(count - 2, rows), hot(count - 1, rows)]),
        ]
    )
    mx = source_mix(x_coupling, col_pos, x_ends_f[0:2], x_ends_f[width + 2 :], n_plane)
    my = source_mix(
        y_coupling, row_pos, jnp.transpose(next_y, (2, 0, 1)), jnp.transpose(prior_y, (2, 0, 1)), n_plane
    )

    def fold_x(a0, a1):
        lap = viscosity * (x_scale * x_scale * a1 + x_curv * a0)
        return jnp.concatenate([lap, x_scale * a0], axis=-1)

    def fold_y(a0, a1):
        return jnp.stack([viscosity * (y_scale * y_scale * a1 + y_curv * a0), y_scale * a0])

    def by_k(basis):
        zero = jnp.zeros_like(basis[0])
        return jnp.concatenate([basis[0], zero]), jnp.concatenate([zero, basis[1]])

    edge = jnp.concatenate([xt[:, 0:2], xt[:, width + 2 :]], axis=1).astype(f32)
    x0, x1 = by_k(x_basis)
    bx8 = fold_x(jnp.concatenate([x0, edge[0]]), jnp.concatenate([x1, edge[1]]))
    y0, y1 = by_k(y_basis[0])
    by8 = jnp.pad(fold_y(y0, y1), ((0, 0), (0, 4), (0, 0)))
    place = jnp.arange(rows + 4, dtype=jnp.int32) - 2
    livek = jnp.logical_and(place < count, jnp.logical_or(place >= 0, row_pos > 0))
    livek = jnp.logical_or(livek, jnp.logical_and(place >= rows, row_pos < n_row - 1))
    livek = livek.astype(f32)[None, :]
    xrow = jnp.stack([x_scale, x_curv])

    thin = -(-(gy * group + tail) // 128) * 128
    sx = np.zeros((n_plane, gx, n_plane, 4, 8), np.float32)
    s1 = np.zeros((8, n_plane, thin), np.float32)
    s2 = np.zeros((128, n_plane, thin), np.float32)
    s3 = np.zeros((tail + 4, n_plane, thin), np.float32)
    for z in range(n_plane):
        for c in range(4):
            sx[z, :n_col, z, c, c] = 1.0
            s1[c, z, np.arange(n_row) * group + z * 4 + c] = 1.0
        for h in range(2):
            sx[z, n_col, z, h, 4 + h] = 1.0
            sx[z, n_col + 1, z, 2 + h, 6 + h] = 1.0
            s2[h, z, n_row * group + z * 4 + h] = 1.0
            s3[tail + 2 + h, z, (n_row + 1) * group + z * 4 + 2 + h] = 1.0
        for t in range(tail):
            s3[2 + t, z, gy * group + t] = 1.0
    sx = jnp.asarray(sx.reshape(-1, 8), bf16)
    s1, s2, s3 = (jnp.asarray(s.reshape(s.shape[0], -1), bf16) for s in (s1, s2, s3))

    xs_row = x_scale.reshape(1, width)
    limit = 60 * 1024 * 1024
    whole = lambda shape: pl.BlockSpec(shape, lambda *i: (0,) * len(shape))
    by_plane = lambda shape: pl.BlockSpec((1,) + shape[1:], lambda z, *i: (z,) + (0,) * (len(shape) - 1))
    fields = pl.BlockSpec((n_comp, 1, rows, width), lambda z, *i: (0, z, 0, 0))
    xo, yo, top = pl.pallas_call(
        stats_kernel,
        name="stats",
        grid=(n_plane,),
        in_specs=[fields] + [whole(a.shape) for a in (dx, dy, mx, my, xs_row, ycol)],
        out_specs=[
            whole((gx, n_comp * group, rows)),
            whole((gy, n_comp * group, width)),
            whole((8, 128)),
        ],
        out_shape=[
            jax.ShapeDtypeStruct((gx, n_comp * group, rows), bf16),
            jax.ShapeDtypeStruct((gy, n_comp * group, width), bf16),
            jax.ShapeDtypeStruct((8, 128), f32),
        ],
        scratch_shapes=[
            pltpu.VMEM((n_comp, n_plane, 8, rows), f32),
            pltpu.VMEM((n_comp, n_plane, 8, width), f32),
            pltpu.VMEM((1, width), f32),
        ],
        compiler_params=pltpu.CompilerParams(vmem_limit_bytes=limit),
    )(velocity, dx, dy, mx, my, xs_row, ycol)

    dma = pltpu.SemaphoreType.DMA
    anywhere = pl.BlockSpec(memory_space=pl.ANY)
    in_vmem = pl.BlockSpec(memory_space=pltpu.VMEM)
    sources = (xt, yt, xrow, ycol, livek, bx8, by8, sx, s1, s2, s3)
    xr, yr, tops, lx, bx, wy, wt = pl.pallas_call(
        functools.partial(exchange_kernel, n_row, n_col),
        name="exchange",
        in_specs=[anywhere] * 3 + [in_vmem] * len(sources),
        out_specs=[anywhere] * 3 + [in_vmem] * 4,
        out_shape=[
            jax.ShapeDtypeStruct(xo.shape, bf16),
            jax.ShapeDtypeStruct(yo.shape, bf16),
            jax.ShapeDtypeStruct((n_row, n_col, 8, 128), f32),
            jax.ShapeDtypeStruct((width, 2 * width), bf16),
            jax.ShapeDtypeStruct((n_plane, gx * group, 2 * width), bf16),
            jax.ShapeDtypeStruct((2, rows, main), bf16),
            jax.ShapeDtypeStruct((n_plane, 2, rows, thin), bf16),
        ],
        scratch_shapes=[
            dma((n_col,)), dma((n_col,)), dma((n_row,)), dma((n_row,)), dma((n_col,)), dma((n_col,)),
            dma((n_row,)), dma((n_row,)), dma((4,)), dma((4,)), dma((3,)),
        ],
        compiler_params=pltpu.CompilerParams(
            collective_id=0, has_side_effects=True, vmem_limit_bytes=limit
        ),
    )(xo, yo, top, *sources)

    one = pl.BlockSpec((1, 1, rows, width), lambda z, f: (f, z, 0, 0))
    tile = 256 if main >= 512 else main
    return pl.pallas_call(
        functools.partial(main_kernel, main, tile),
        name="sub_step",
        grid=(n_plane, n_comp),
        in_specs=[
            fields,
            one,
            pl.BlockSpec((gx, group, rows), lambda z, f: (0, f, 0)),
            pl.BlockSpec((gy, group, width), lambda z, f: (0, f, 0)),
            whole(lx.shape),
            by_plane(bx.shape),
            whole(wy.shape),
            by_plane(wt.shape),
            whole(tops.shape),
            whole(ycol.shape),
        ],
        out_specs=[one, one],
        out_shape=[jax.ShapeDtypeStruct(velocity.shape, bf16)] * 2,
        scratch_shapes=[pltpu.VMEM((thin, width), bf16)],
        compiler_params=pltpu.CompilerParams(vmem_limit_bytes=limit),
    )(velocity, rhs_prev, xr, yr, lx, bx, wy, wt, tops, ycol)


def solution(mesh):
    placed = (
        P(None, None, "row", "col"),
        P(None, None, "row", "col"),
        P(),
        P("col"),
        P("col"),
        P("row"),
        P("row"),
        P(),
        P(),
        P(),
        P("row", None, None),
        P(),
        P("row", None, None, None),
    )
    return jax.shard_map(
        shards,
        mesh=mesh,
        in_specs=placed,
        out_specs=(P(None, None, "row", "col"), P(None, None, "row", "col")),
        check_vma=False,
    )
```
